32 devices in a mesh: grp: 4 (over x, core), mem: 8 (over z, y).
Axes of the slice: x: 2, y: 2, z: 4, core: 2. Of those that a mesh axis runs over, the one named last changes fastest.
Arguments:
- slab: float32 [1024, 4096], P('mem', 'grp'), may hold values from 0 to 32, as said below
- tiles: float32 [4096, 4096], P('grp', 'mem'), may hold values from 0 to 1.05, as said below
- slot_rows: int32 [8, 8], P('grp'), may hold values from -1 to 1, as said below
Outputs:
- clustered: float32 [1024, 4096], P('grp', 'mem')
The draws below stay inside these ranges and needn't reach their ends.
Inputs may be any that keep to these rules, and one draw needn't show every extreme that they name: For each group g and block column m, the used slots h (slot_rows[g * 2 + h, m] >= 0) come first and name distinct block rows of the group; unused slots hold -1. Each block column has at least one used slot in every group, and in every draw some group and block column has all 2 slots used. Entries are nonnegative, positive in the tiles of used slots, and zero in the tiles of unused slots. `slab`: entries are positive.
All inputs are finite; a program needn't handle non-finite values.
Results may differ from the reference program's by a relative error of at most 0.0003.
Values sent between devices are 32-bit elements; how exact they have to be, the bound alone decides.
No kernel may reach another device: no remote copies, remote signals or barrier semaphores. Data moves between devices by JAX's collectives and lax.ppermute only.
A program may use at most 64 MiB of HBM per device.

```python
import jax
import jax.numpy as jnp
from jax import lax

TILE = 512
HELD = 2
GROUPS = 4
MEMBERS = 8
GROUP_BLOCKS = 2
NCOLS = 4096
WROWS = 1024


def slot_layout(key):
    anchor = jax.random.fold_in(key, 7)
    device_count = GROUPS * MEMBERS
    device_keys = jax.random.split(anchor, device_count)
    orders = jax.vmap(lambda subkey: jax.random.permutation(subkey, GROUP_BLOCKS)[:HELD])(device_keys)
    counts = jax.random.randint(jax.random.fold_in(anchor, 1), (device_count,), 1, HELD + 1)
    chosen_full = jax.random.randint(jax.random.fold_in(anchor, 2), (), 0, device_count)
    counts = jnp.where(jnp.arange(device_count) == chosen_full, HELD, counts)
    slot_ids = jnp.arange(HELD)[None, :]
    row_table = jnp.where(slot_ids < counts[:, None], orders, -1)
    row_table = row_table.reshape(GROUPS, MEMBERS, HELD).transpose(0, 2, 1).reshape(GROUPS * HELD, MEMBERS)
    return row_table.astype(jnp.int32)


def draw_slot_rows(key, part):
    return slot_layout(key)


def draw_tiles(key, part):
    layout = slot_layout(key)
    filled = (layout >= 0).astype(jnp.float32)
    values = jax.random.uniform(jax.random.fold_in(key, 11), (GROUPS * HELD * TILE, NCOLS), jnp.float32)
    entries = jnp.exp(jnp.log(0.01) + values * jnp.log(100.0))
    expand_mask = jnp.repeat(jnp.repeat(filled, TILE, axis=0), TILE, axis=1)
    return entries * expand_mask


def draw_slab(key, part):
    values = jax.random.uniform(jax.random.fold_in(key, 21), (WROWS, NCOLS), jnp.float32)
    scale_draw = jax.random.uniform(jax.random.fold_in(key, 22), (WROWS, 1), jnp.float32)
    position = jnp.arange(WROWS, dtype=jnp.float32)[:, None] / WROWS
    row_scale = jnp.exp(scale_draw * jnp.log(10.0)) * jnp.exp(position * jnp.log(3.0))
    entries = jnp.exp(jnp.log(0.01) + values * jnp.log(100.0))
    return entries * row_scale


def setup_inputs(seed: int = 0) -> dict:
    key_list = jax.random.split(jax.random.key(seed), 4)
    return {
        "slab": draw_slab(jax.random.fold_in(key_list[3], 71), 0),
        "tiles": draw_tiles(jax.random.fold_in(key_list[3], 71), 0),
        "slot_rows": draw_slot_rows(jax.random.fold_in(key_list[3], 71), 0),
    }


def column_block(member, slab, tiles, slot_rows):
    tile_column = lax.dynamic_slice_in_dim(tiles, member * TILE, TILE, 1).reshape(GROUPS * HELD, TILE, TILE)
    local_rows = lax.dynamic_index_in_dim(slot_rows, member, axis=1, keepdims=False)
    group_ids = jnp.repeat(jnp.arange(GROUPS, dtype=jnp.int32), HELD)
    block_ids = (group_ids * GROUP_BLOCKS + jnp.maximum(local_rows, 0)).astype(jnp.int32)
    slab_blocks = slab.reshape(WROWS, MEMBERS, TILE)
    chosen = jnp.take(slab_blocks, block_ids, axis=1)
    return jnp.einsum("wst,stu->wu", chosen, tile_column, precision=lax.Precision.HIGHEST)


def reference(slab, tiles, slot_rows):
    members = jnp.arange(MEMBERS, dtype=jnp.int32)
    blocks = lax.map(lambda member: column_block(member, slab, tiles, slot_rows), members)
    expanded = jnp.transpose(blocks, (1, 0, 2)).reshape(WROWS, NCOLS)
    inflated = expanded * expanded
    column_means = jnp.sum(inflated, axis=0) / WROWS
    return inflated / column_means
```

```python
import jax
import jax.numpy as jnp
from jax import lax
from jax.sharding import PartitionSpec as P

CORES = 2
PIECES = 2


def make_per_device(groups, members):
    planes = groups
    span = members // planes
    chips = groups // CORES

    ring = [(z * span + y, (z - 1) % planes * span + y) for z in range(planes) for y in range(span)]
    turn = [(z * span + y, z * span + (y - 1) % span) for z in range(planes) for y in range(span)]

    def flat(chip, core, member):
        return (chip * CORES + core) * members + member

    def to_core(step):
        pairs = []
        for member in range(members):
            core = (member // span + step) % planes % CORES
            for chip in range(chips):
                pairs += [(flat(chip, c, member), flat(chip, core, member)) for c in range(CORES) if c != core]
        return pairs

    def across_chips(step, shift):
        pairs = []
        for member in range(members):
            core = (member // span + step) % planes % CORES
            pairs += [(flat(x, core, member), flat((x + shift) % chips, core, member)) for x in range(chips)]
        return pairs

    swap = [(x * CORES + c, x * CORES + (c + 1) % CORES) for x in range(chips) for c in range(CORES)]

    def per_device(slab, tiles, slot_rows):
        tile_size = tiles.shape[1]
        slot_total = tiles.shape[0] // tile_size
        rows, depth = slab.shape
        group = lax.axis_index("grp")
        member = lax.axis_index("mem")
        plane, place = member // span, member % span
        own_rows = lax.dynamic_index_in_dim(slot_rows, member, axis=1, keepdims=False)
        tile_stack = tiles.reshape(slot_total, tile_size, tile_size)
        blocks = []
        for block in range(depth // tile_size):
            blocks.append(sum(jnp.where(own_rows[h] == block, tile_stack[h], 0.0) for h in range(slot_total)))
        column = jnp.concatenate(blocks, 0)

        part = rows // PIECES
        pieces = {}
        for p in range(PIECES):
            held = slab[p * part : (p + 1) * part]
            for step in range(planes):
                if step:
                    held = lax.ppermute(held, "mem", ring)
                pieces[step, p, 0] = held
        for step in range(planes):
            for p in range(PIECES):
                for s in range(1, span):
                    pieces[step, p, s] = lax.ppermute(pieces[step, p, s - 1], "mem", turn)

        kept = jnp.zeros((span, rows, tile_size), jnp.float32)
        sums = jnp.zeros((tile_size,), jnp.float32)
        for step in range(planes):
            stack = jnp.concatenate([pieces[step, p, s] for s in range(span) for p in range(PIECES)], 0)
            partial = jnp.dot(stack, column, precision=lax.Precision.HIGH, preferred_element_type=jnp.float32)
            merged = partial + lax.ppermute(partial, ("grp", "mem"), to_core(step))
            total = merged
            for shift in range(1, chips):
                total = total + lax.ppermute(merged, ("grp", "mem"), across_chips(step, shift))
            source = (plane + step) % planes
            square = total * total
            sums = sums + jnp.where(source % CORES == group % CORES, jnp.sum(square, 0), 0.0)
            kept = jnp.where(source == group, square.reshape(span, rows, tile_size), kept)
        column_sums = sums + lax.ppermute(sums, "grp", swap)
        kept = jnp.roll(kept, place, axis=0)
        column_means = column_sums / (rows * members)
        return kept.reshape(span * rows, tile_size) / column_means

    return per_device


def solution(mesh):
    return jax.shard_map(
        make_per_device(mesh.shape["grp"], mesh.shape["mem"]),
        mesh=mesh,
        in_specs=(P("mem", "grp"), P("grp", "mem"), P("grp", None)),
        out_specs=P("grp", "mem"),
        check_vma=False,
    )
```
